128 devices in a mesh: tile: 8 (over z, core), orbit: 16 (over y, x).
Axes of the slice: x: 4, y: 4, z: 4, core: 2. Of those that a mesh axis runs over, the one named last changes fastest.
Arguments:
- jacobians: bfloat16 [16384, 128, 3, 128], P(('tile', 'orbit')), may hold values from -1.5 to 1.5
- point_normals: float32 [16384, 6, 128], P(('tile', 'orbit')), as said below
- block_counts: int32 [128, 128], P(('tile', 'orbit')), may hold values from 1 to 128, 8192 in all within a row
- pair_owner: int32 [16384, 1], P(('tile', 'orbit')), may hold values from 0 to 15; in each aligned block of 128 rows (0 to 127, 128 to 255, ...) at most 16 rows name the same one
- pair_local: int32 [16384], P(('tile', 'orbit')), may hold values from 0 to 255
- crossing: int32 [16], replicated, may hold values from 0 to 15, as said below
Outputs:
- coupled: float32 [16, 256, 4096], P('orbit', 'tile')
The draws below stay inside these ranges and needn't reach their ends.
Inputs may be any that keep to these rules, and one draw needn't show every extreme that they name: `point_normals`: each 3x3 block is symmetric, and in every row the diagonal entry exceeds the sum of the off-diagonal magnitudes by 0.2 or more. `pair_owner`: among the 128 rows of one device no owner appears more than 16 times. crossing[crossing[o]] = o and crossing[o] != o for every orbit o.
All inputs are finite; a program needn't handle non-finite values.
Results may differ from the reference program's by a relative error of at most 0.0029.
Values sent between devices are 32-bit elements; how exact they have to be, the bound alone decides.
No kernel may reach another device: no remote copies, remote signals or barrier semaphores. Data moves between devices by JAX's collectives and lax.ppermute only.
A program may use at most 128 MiB of HBM per device.

```python
import math
import jax
import jax.numpy as jnp
import numpy as np
from jax import lax

P_SIZE = 64
PTS = 128
SLOT_DEV = 128
PAIR_ORB = 256
ORBITS = 16
GROUPS = 128
SLOTS_ALL = 16384
NPAIR = 4096
CAP = 16


def draw_point_normals(key, part):
    key_diag, key_off = jax.random.split(key)
    diagonal = 1.2 + 0.6 * jax.random.uniform(key_diag, (SLOTS_ALL, 3, PTS), jnp.float32)
    off_part = jax.random.uniform(key_off, (SLOTS_ALL, 3, PTS), jnp.float32, -0.5, 0.5)
    return jnp.concatenate([diagonal, off_part], axis=1).astype(jnp.float32)


def draw_crossing(key, part):
    order = jax.random.permutation(key, ORBITS).astype(jnp.int32)
    partner_pos = jnp.arange(ORBITS, dtype=jnp.int32) ^ 1
    return jnp.zeros((ORBITS,), jnp.int32).at[order].set(order[partner_pos])


def with_ends(values, stream_key, smallest, largest):
    longest = values.shape.index(max(values.shape))
    spots = []
    for shift in (0, 1):
        where = [jax.random.randint(jax.random.fold_in(stream_key, axis), (), 0, length) for axis, length in enumerate(values.shape)]
        where[longest] = (where[longest] + shift) % values.shape[longest]
        spots.append(tuple(where))
    return values.at[spots[0]].set(smallest).at[spots[1]].set(largest)


def shard_levels(own_key, shape, shards, low, largest):
    gain = 1.0
    for position, blocks in shards:
        heights = jax.random.uniform(jax.random.fold_in(jax.random.fold_in(own_key, 6), position), (blocks,), jnp.float32, low / len(shards), largest / len(shards))
        gain = gain * jnp.repeat(jnp.exp(heights), shape[position] // blocks).reshape((-1,) + (1,) * (len(shape) - 1 - position))
    return gain


def split_up(number_of, total, most, lean):
    weights = [(1 << 20) // math.isqrt(rank ** lean) + 1 for rank in range(2, number_of + 1)]
    rest, given = total - most - (number_of - 1), [1] * (number_of - 1)
    while rest > 0:
        candidates = [i for i in range(number_of - 1) if given[i] < most]
        whole, budget = sum([weights[i] for i in candidates]), rest
        for i in candidates:
            more = min(most - given[i], max(1, budget * weights[i] // whole), rest)
            given[i] = given[i] + more
            rest = rest - more
    return np.array([most] + given)


def ragged_sizes(own_key, number_of, total, most, skew):
    if number_of == 2:
        one = jax.random.randint(own_key, (), max(1, total - most), min(most, total - 1) + 1)
        return jnp.stack([one, total - one])
    tallies = jnp.asarray(split_up(number_of, total, most, skew), jnp.int32)
    pairs = (number_of - 1) // 2
    source_of, receiver = tallies[1:1 + 2 * pairs:2], tallies[2:2 + 2 * pairs:2]
    slack = jnp.minimum(source_of - 1, most - receiver)
    passed = jax.random.randint(jax.random.fold_in(own_key, 1), (pairs,), 0, 1 << 20) % (slack + 1)
    tallies = tallies.at[1:1 + 2 * pairs:2].set(source_of - passed).at[2:2 + 2 * pairs:2].set(receiver + passed)
    return tallies[jax.random.permutation(jax.random.fold_in(own_key, 2), number_of)]


def assign_block(rng, own, number, rows, number_of, top, reach, lean):
    order = jax.random.permutation(rng, number_of)
    packed, common = load_shares(number_of, rows * top, reach, lean, True), load_shares(number_of, rows * top, reach, lean, False)
    places = jnp.arange(number_of)

    def named(lengths, offset_by):
        used = int((lengths > 0).sum())
        fixed = max(1, used // 4)
        passed = fixed + (places - fixed + offset_by * (used - fixed)) % max(1, number_of - fixed)
        return jnp.zeros((number_of,), jnp.int32).at[order[jnp.where(places < fixed, places, passed)]].set(jnp.asarray(lengths, jnp.int32))

    lengths = jnp.where(number % 4 == 0, named(packed, number // 4), named(common, number - number // 4 - 1))
    mixed = jax.random.permutation(jax.random.fold_in(own, 3), number_of)
    donor, sink = mixed[0:number_of // 2 * 2:2], mixed[1:number_of // 2 * 2:2]
    margin = jnp.minimum(lengths[donor] - 1, reach - lengths[sink]) // 2
    margin = jnp.where((donor == order[0]) | (sink == order[0]) | (lengths[sink] == 0), 0, jnp.maximum(margin, 0))
    passed = jax.random.randint(jax.random.fold_in(own, 4), (number_of // 2,), 0, 1 << 20) % (margin + 1)
    lengths = lengths.at[donor].add(-passed).at[sink].add(passed)
    items = jnp.searchsorted(jnp.cumsum(lengths), jnp.arange(rows * top), side="right").astype(jnp.int32)
    grid = items.reshape(top, rows).T
    grid = grid[jax.random.permutation(jax.random.fold_in(own, 1), rows)]
    offset_by = jax.random.randint(jax.random.fold_in(own, 2), (rows, 1), 0, top)
    return jnp.take_along_axis(grid, (jnp.arange(top)[None, :] + offset_by) % top, axis=1)


def load_shares(count, total, bound, slope, full):
    portions = [(1 << 20) // math.isqrt(rank ** slope) + 1 for rank in range(1, count + 1)]
    largest = bound if full else min(bound, max(-(-total // count), total * portions[0] // sum(portions)))
    least = 1 if total - largest >= count - 1 else 0
    given, spare = [largest] + [least] * (count - 1), total - largest - least * (count - 1)
    while spare > 0:
        movable = [i for i in range(1, count) if given[i] < largest] or [i for i in range(1, count) if given[i] < bound]
        mass, left = sum([portions[i] for i in movable]), spare
        for i in movable:
            extra = min(bound - given[i], max(1, left * portions[i] // mass), spare)
            given[i] = given[i] + extra
            spare = spare - extra
    return np.array(given)


def scatter_about(key, shape, scale, reach, shards=(), held_as=jnp.bfloat16):
    values = jax.random.normal(key, shape, jnp.float32) * scale
    if len(shards) > 0:
        values = shard_levels(key, shape, shards, -0.22, 0.18) * values
    return jnp.clip(values, min=-reach, max=reach).astype(held_as)


def setup_inputs(seed: int = 0) -> dict:
    streams_of = jax.random.split(jax.random.key(seed), 7)
    jacobians = scatter_about(streams_of[0], (SLOTS_ALL, PTS, 3, 2 * P_SIZE), 0.25, 1.5, ((0, 128),))
    point_normals = draw_point_normals(jax.random.fold_in(streams_of[6], 71), 0)
    block_counts = jax.vmap(lambda own: ragged_sizes(own, SLOT_DEV, SLOT_DEV * PTS // 2, PTS, 2))(jax.random.split(streams_of[2], GROUPS)).reshape((GROUPS, SLOT_DEV)).astype(jnp.int32)
    pair_owner_keys = jax.random.split(jax.random.fold_in(streams_of[3], 1), SLOTS_ALL // SLOT_DEV)
    pair_owner_turns = jax.random.permutation(jax.random.fold_in(streams_of[3], 3), SLOTS_ALL // SLOT_DEV)
    pair_owner = jax.vmap(lambda own, number: assign_block(jax.random.fold_in(streams_of[3], 2), own, number, SLOT_DEV, ORBITS, 1, CAP, 2))(pair_owner_keys, pair_owner_turns).reshape((SLOTS_ALL, 1))
    pair_local = with_ends(jax.random.randint(streams_of[4], (SLOTS_ALL,), 0, PAIR_ORB), jax.random.fold_in(streams_of[4], 1), 0, PAIR_ORB - 1).astype(jnp.int32)
    crossing = draw_crossing(jax.random.fold_in(streams_of[6], 71), 0)
    return dict(jacobians=jacobians, point_normals=point_normals, block_counts=block_counts, pair_owner=pair_owner, pair_local=pair_local, crossing=crossing)


def eliminate(jacobians, point_normals, counts):
    jac_float = jacobians.astype(jnp.float32)
    left_half = jac_float[..., :P_SIZE]
    right_half = jac_float[..., P_SIZE:]
    diag_one = point_normals[:, 0, :][:, :, None]
    diag_two = point_normals[:, 1, :][:, :, None]
    diag_three = point_normals[:, 2, :][:, :, None]
    off_ab = point_normals[:, 3, :][:, :, None]
    off_ac = point_normals[:, 4, :][:, :, None]
    off_bc = point_normals[:, 5, :][:, :, None]
    cof_aa = diag_two * diag_three - off_bc * off_bc
    cof_bb = diag_one * diag_three - off_ac * off_ac
    cof_cc = diag_one * diag_two - off_ab * off_ab
    cof_ab = off_ac * off_bc - off_ab * diag_three
    cof_ac = off_ab * off_bc - off_ac * diag_two
    cof_bc = off_ab * off_ac - diag_one * off_bc
    determinant = diag_one * cof_aa + off_ab * cof_ab + off_ac * cof_ac
    live_mask = (jnp.arange(PTS, dtype=jnp.int32)[None, :] < counts[:, None]).astype(jnp.float32)
    weight = live_mask[:, :, None] / determinant
    comp_a = right_half[:, :, 0, :]
    comp_b = right_half[:, :, 1, :]
    comp_c = right_half[:, :, 2, :]
    solved = jnp.stack([
        (cof_aa * comp_a + cof_ab * comp_b + cof_ac * comp_c) * weight,
        (cof_ab * comp_a + cof_bb * comp_b + cof_bc * comp_c) * weight,
        (cof_ac * comp_a + cof_bc * comp_b + cof_cc * comp_c) * weight], axis=2)
    solved = lax.optimization_barrier(solved.astype(jnp.bfloat16))
    blocks = jnp.einsum("spci,spcj->sij", left_half, solved.astype(jnp.float32))
    return blocks.reshape(blocks.shape[0], P_SIZE * P_SIZE)


def one_device(pieces):
    return eliminate(pieces[0], pieces[1], pieces[2])


def reference(jacobians, point_normals, block_counts, pair_owner, pair_local, crossing):
    device_jac = jacobians.reshape(GROUPS, SLOT_DEV, PTS, 3, 2 * P_SIZE)
    device_normals = point_normals.reshape(GROUPS, SLOT_DEV, 6, PTS)
    blocks = lax.map(one_device, (device_jac, device_normals, block_counts))
    blocks = blocks.reshape(SLOTS_ALL, P_SIZE * P_SIZE)
    pair_ids = (pair_owner[:, 0] * PAIR_ORB + pair_local).astype(jnp.int32)
    reduced = jax.ops.segment_sum(blocks, pair_ids, num_segments=NPAIR)
    reduced = reduced.reshape(ORBITS, PAIR_ORB, P_SIZE, P_SIZE)
    mirror = jnp.swapaxes(reduced[crossing], 2, 3)
    return (reduced + mirror).reshape(ORBITS, PAIR_ORB, P_SIZE * P_SIZE)
```

```python
import functools

import jax
import jax.numpy as jnp
from jax import lax
from jax.experimental import pallas as pl
from jax.experimental.pallas import tpu as pltpu
from jax.sharding import PartitionSpec as P

DEVICES = 128
SLOTS = 128
PTS = 128
PARAMS = 64
ORBITS = 16
PAIR_ORB = 256
TILES = 8
ELEMS = PARAMS * PARAMS // DEVICES
ROWS = ELEMS + 1
STEP_SLOTS = 8
STEP_SRC = 16
NT = (((1,), (1,)), ((), ()))


def dot_nt(a, b):
    return lax.dot_general(a, b, NT, preferred_element_type=jnp.float32)


def eye(n):
    r = lax.broadcasted_iota(jnp.int32, (n, n), 0)
    c = lax.broadcasted_iota(jnp.int32, (n, n), 1)
    return jnp.where(r == c, 1.0, 0.0).astype(jnp.bfloat16)


def crossing_ranks(cross, ranks):
    seen = jnp.int32(0)
    for o in range(ORBITS):
        ranks[o] = seen
        seen = seen + (cross[o] > o).astype(jnp.int32)


def pair_of(o, cross, ranks):
    return ranks[jnp.minimum(o, cross[o])]


def blocks_kernel(counts, owner, cross, jac, normals, owner_row, local_row, out, held, ranks):
    step = pl.program_id(0)
    w11, w22, w33 = normals[0], normals[1], normals[2]
    w12, w13, w23 = normals[3], normals[4], normals[5]
    c11 = w22 * w33 - w23 * w23
    c22 = w11 * w33 - w13 * w13
    c33 = w11 * w22 - w12 * w12
    c12 = w13 * w23 - w12 * w33
    c13 = w12 * w23 - w13 * w22
    c23 = w12 * w13 - w11 * w23
    det = w11 * c11 + w12 * c12 + w13 * c13
    sub = lax.broadcasted_iota(jnp.int32, (STEP_SLOTS, PTS), 0)
    place = lax.broadcasted_iota(jnp.int32, (STEP_SLOTS, PTS), 1)
    limit = jnp.zeros((STEP_SLOTS, PTS), jnp.int32)
    for i in range(STEP_SLOTS):
        limit = jnp.where(sub == i, counts[step * STEP_SLOTS + i], limit)
    weight = jnp.where(place < limit, 1.0, 0.0) / det
    c11, c22, c33 = c11 * weight, c22 * weight, c33 * weight
    c12, c13, c23 = c12 * weight, c13 * weight, c23 * weight
    ident = eye(2 * PARAMS)
    for i in range(STEP_SLOTS):
        slot = step * STEP_SLOTS + i
        turned = dot_nt(ident, jac[i])
        left = turned[:PARAMS].astype(jnp.bfloat16)
        right = turned[PARAMS:]
        one, two, three = right[:, :PTS], right[:, PTS : 2 * PTS], right[:, 2 * PTS :]
        row = slice(i, i + 1)
        solved = jnp.concatenate(
            [
                c11[row] * one + c12[row] * two + c13[row] * three,
                c12[row] * one + c22[row] * two + c23[row] * three,
                c13[row] * one + c23[row] * two + c33[row] * three,
            ],
            axis=1,
        ).astype(jnp.bfloat16)
        mine = owner[slot]
        upper = mine > cross[mine]
        a = jnp.where(upper, left, solved)
        b = jnp.where(upper, solved, left)
        held[pl.ds(slot, PARAMS, stride=SLOTS), :] = dot_nt(a, b)

    @pl.when(step == pl.num_programs(0) - 1)
    def _():
        small = eye(PARAMS)
        half = PARAMS // 2
        for col in range(PARAMS):
            lines = held[col * SLOTS : (col + 1) * SLOTS, :].astype(jnp.bfloat16)
            start = (col // half) * PARAMS * ROWS + col % half
            out[pl.ds(start, PARAMS, stride=ROWS), :] = dot_nt(small, lines)
        crossing_ranks(cross, ranks)
        names = owner_row[...]
        ids = jnp.zeros_like(names)
        for o in range(ORBITS):
            ids = jnp.where(names == o, pair_of(o, cross, ranks) * PAIR_ORB, ids)
        ids = (ids + local_row[...]).astype(jnp.float32)
        out[pl.ds(ELEMS, DEVICES, stride=ROWS), :] = jnp.broadcast_to(ids, (DEVICES, SLOTS))


def sum_kernel(cross, arrived, out, hot, values, total, ranks):
    step = pl.program_id(0)

    @pl.when(step == 0)
    def _():
        total[...] = jnp.zeros_like(total)

    lines = lax.broadcasted_iota(jnp.int32, (PAIR_ORB, SLOTS), 0)
    for i in range(STEP_SRC):
        base = i * ROWS
        piece = arrived[base : base + ELEMS, :]
        ids = arrived[base + ELEMS : base + ROWS, :].astype(jnp.int32)
        local = ids & (PAIR_ORB - 1)
        line = (ids >> 8) * 32 + (local >> 6) * 8 + (local & 7)
        group = (local >> 3) & 7
        at = slice(i * SLOTS, (i + 1) * SLOTS)
        hot[:, at] = jnp.where(lines == line, 1.0, 0.0).astype(jnp.bfloat16)
        for g in range(8):
            values[g * ELEMS : (g + 1) * ELEMS, at] = jnp.where(group == g, piece, 0.0).astype(jnp.bfloat16)
    total[...] += dot_nt(hot[...], values[...])

    @pl.when(step == pl.num_programs(0) - 1)
    def _():
        crossing_ranks(cross, ranks)
        for o in range(ORBITS):
            pair = pair_of(o, cross, ranks)
            for t in range(TILES):
                start = pl.multiple_of(pair * 32 + (t >> 1) * 8, 8)
                dest = (t * ORBITS + o) * 8
                out[dest : dest + 8, :] = total[pl.ds(start, 8), (t & 1) * 128 : (t & 1) * 128 + 128]


def place_kernel(cross, arrived, out, turned):
    me = lax.axis_index("orbit")
    upper = me > cross[me]
    lane = lax.broadcasted_iota(jnp.int32, (8, 128), 1)

    @pl.when(jnp.logical_not(upper))
    def _():
        band = lane // 32
        for tile in range(32):
            v = []
            for g in range(4):
                d = (g % 2) * PARAMS + 2 * tile + g // 2
                v.append(arrived[d * 8 : d * 8 + 8, :])
            moved = []
            for r in range(4):
                z = v[r]
                for h in range(1, 4):
                    z = jnp.where(band == h, v[(h + r) % 4], z)
                moved.append(z if r == 0 else pltpu.roll(z, 32 * r, 1))
            for h in range(4):
                u = moved[(0 - h) % 4]
                for g in range(1, 4):
                    u = jnp.where(band == g, moved[(g - h) % 4], u)
                start = (h * 32 + tile) * 8
                out[start : start + 8, :] = u

    @pl.when(upper)
    def _():
        low = lax.broadcasted_iota(jnp.int32, (64, 128), 1) < PARAMS
        for j in range(8):
            turned[...] = arrived[pl.ds(j, 128, stride=8), :].T
            even = turned[pl.ds(0, 64, stride=2), :]
            odd = turned[pl.ds(1, 64, stride=2), :]
            halves = (
                jnp.where(low, even, pltpu.roll(odd, PARAMS, 1)),
                jnp.where(low, pltpu.roll(even, PARAMS, 1), odd),
            )
            for h in range(4):
                for half in range(2):
                    start = h * 256 + half * 128 + j
                    out[pl.ds(start, 16, stride=8), :] = halves[half][h * 16 : h * 16 + 16]


def smem():
    return pl.BlockSpec(memory_space=pltpu.SMEM)


def exchange(x):
    return lax.all_to_all(x, ("tile", "orbit"), split_axis=0, concat_axis=0, tiled=True)


def make_blocks(jacobians, point_normals, counts, owners, locals_, crossing):
    jac = jnp.transpose(jacobians, (0, 2, 1, 3)).reshape(SLOTS, 3 * PTS, 2 * PARAMS)
    normals = jnp.transpose(point_normals, (1, 0, 2))
    row = pl.BlockSpec((1, SLOTS), lambda i: (0, 0))
    return pl.pallas_call(
        blocks_kernel,
        grid=(SLOTS // STEP_SLOTS,),
        in_specs=[
            smem(),
            smem(),
            smem(),
            pl.BlockSpec((STEP_SLOTS, 3 * PTS, 2 * PARAMS), lambda i: (i, 0, 0)),
            pl.BlockSpec((6, STEP_SLOTS, PTS), lambda i: (0, i, 0)),
            row,
            row,
        ],
        out_specs=pl.BlockSpec((DEVICES * ROWS, SLOTS), lambda i: (0, 0)),
        out_shape=jax.ShapeDtypeStruct((DEVICES * ROWS, SLOTS), jnp.float32),
        scratch_shapes=[
            pltpu.VMEM((PARAMS * SLOTS, PARAMS), jnp.float32),
            pltpu.SMEM((ORBITS,), jnp.int32),
        ],
        name="blocks",
    )(counts, owners, crossing, jac, normals, owners.reshape(1, SLOTS), locals_.reshape(1, SLOTS))


def sum_pairs(arrived, crossing):
    return pl.pallas_call(
        sum_kernel,
        grid=(DEVICES // STEP_SRC,),
        in_specs=[smem(), pl.BlockSpec((STEP_SRC * ROWS, SLOTS), lambda i: (i, 0))],
        out_specs=pl.BlockSpec((DEVICES * 8, 128), lambda i: (0, 0)),
        out_shape=jax.ShapeDtypeStruct((DEVICES * 8, 128), jnp.float32),
        scratch_shapes=[
            pltpu.VMEM((PAIR_ORB, STEP_SRC * SLOTS), jnp.bfloat16),
            pltpu.VMEM((PAIR_ORB, STEP_SRC * SLOTS), jnp.bfloat16),
            pltpu.VMEM((PAIR_ORB, PAIR_ORB), jnp.float32),
            pltpu.SMEM((ORBITS,), jnp.int32),
        ],
        name="sum_pairs",
    )(crossing, arrived)


def place(arrived, crossing):
    return pl.pallas_call(
        place_kernel,
        in_specs=[smem(), pl.BlockSpec(memory_space=pltpu.VMEM)],
        out_specs=pl.BlockSpec(memory_space=pltpu.VMEM),
        out_shape=jax.ShapeDtypeStruct((DEVICES * 8, 128), jnp.float32),
        scratch_shapes=[pltpu.VMEM((128, 128), jnp.float32)],
        name="place",
    )(crossing, arrived)


def local(jacobians, point_normals, block_counts, pair_owner, pair_local, crossing):
    sent = make_blocks(
        jacobians, point_normals, block_counts.reshape(SLOTS), pair_owner.reshape(SLOTS), pair_local, crossing
    )
    arrived = exchange(sent.reshape(DEVICES, ROWS, 1, SLOTS))
    sums = sum_pairs(arrived.reshape(DEVICES * ROWS, SLOTS), crossing)
    mine = exchange(sums.reshape(DEVICES, 8, 128))
    out = place(mine.reshape(DEVICES * 8, 128), crossing)
    out = jnp.transpose(out.reshape(4, 32, 8, 128), (0, 2, 1, 3))
    return out.reshape(1, PAIR_ORB // TILES, PARAMS * PARAMS)


def solution(mesh):
    both = ("tile", "orbit")
    in_specs = (
        P(both, None, None, None),
        P(both, None, None),
        P(both, None),
        P(both, None),
        P(both),
        P(),
    )
    return jax.shard_map(local, mesh=mesh, in_specs=in_specs, out_specs=P("orbit", "tile", None), check_vma=False)
```

```python
import jax
import jax.numpy as jnp
from jax import lax
from jax.experimental import pallas as pl
from jax.experimental.pallas import tpu as pltpu
from jax.sharding import PartitionSpec as P

DEVICES = 128
SLOTS = 128
PTS = 128
PARAMS = 64
ORBITS = 16
PAIR_ORB = 256
TILES = 8
ELEMS = PARAMS * PARAMS // DEVICES
ROWS = ELEMS + 1
STEP_SLOTS = 8
STEP_SRC = 16
NT = (((1,), (1,)), ((), ()))


def dot_nt(a, b):
    return lax.dot_general(a, b, NT, preferred_element_type=jnp.float32)


def eye(n):
    r = lax.broadcasted_iota(jnp.int32, (n, n), 0)
    c = lax.broadcasted_iota(jnp.int32, (n, n), 1)
    return jnp.where(r == c, 1.0, 0.0).astype(jnp.bfloat16)


def crossing_ranks(cross, ranks):
    seen = jnp.int32(0)
    for o in range(ORBITS):
        ranks[o] = seen
        seen = seen + (cross[o] > o).astype(jnp.int32)


def pair_of(o, cross, ranks):
    return ranks[jnp.minimum(o, cross[o])]


def blocks_kernel(counts, owner, cross, jac_hbm, normals_hbm, owner_row, local_row, out, jac, normals, held, ranks, sems):
    steps = SLOTS // STEP_SLOTS
    copy_normals = pltpu.make_async_copy(normals_hbm, normals, sems.at[steps])
    copy_normals.start()

    def part(step):
        at = pl.ds(step * STEP_SLOTS, STEP_SLOTS)
        return pltpu.make_async_copy(jac_hbm.at[at], jac.at[at], sems.at[step])

    for step in range(steps):
        part(step).start()
    crossing_ranks(cross, ranks)
    names = owner_row[...]
    ids = jnp.zeros_like(names)
    for o in range(ORBITS):
        ids = jnp.where(names == o, pair_of(o, cross, ranks) * PAIR_ORB, ids)
    ids = (ids + local_row[...]).astype(jnp.float32)
    out[pl.ds(ELEMS, DEVICES, stride=ROWS), :] = jnp.broadcast_to(ids, (DEVICES, SLOTS))
    copy_normals.wait()
    sub = lax.broadcasted_iota(jnp.int32, (STEP_SLOTS, PTS), 0)
    place = lax.broadcasted_iota(jnp.int32, (STEP_SLOTS, PTS), 1)

    def body(step, carry):
        base = pl.multiple_of(step * STEP_SLOTS, STEP_SLOTS)
        w11, w22, w33, w12, w13, w23 = (normals[q, pl.ds(base, STEP_SLOTS), :] for q in range(6))
        c11 = w22 * w33 - w23 * w23
        c22 = w11 * w33 - w13 * w13
        c33 = w11 * w22 - w12 * w12
        c12 = w13 * w23 - w12 * w33
        c13 = w12 * w23 - w13 * w22
        c23 = w12 * w13 - w11 * w23
        det = w11 * c11 + w12 * c12 + w13 * c13
        limit = jnp.zeros((STEP_SLOTS, PTS), jnp.int32)
        for i in range(STEP_SLOTS):
            limit = jnp.where(sub == i, counts[base + i], limit)
        weight = jnp.where(place < limit, 1.0, 0.0) / det
        c11, c22, c33 = c11 * weight, c22 * weight, c33 * weight
        c12, c13, c23 = c12 * weight, c13 * weight, c23 * weight
        part(step).wait()
        for i in range(STEP_SLOTS):
            slot = base + i
            turned = jac[slot].T
            left = turned[:PARAMS]
            right = turned[PARAMS:].astype(jnp.float32)
            one, two, three = right[:, :PTS], right[:, PTS : 2 * PTS], right[:, 2 * PTS :]
            row = slice(i, i + 1)
            solved = jnp.concatenate(
                [
                    c11[row] * one + c12[row] * two + c13[row] * three,
                    c12[row] * one + c22[row] * two + c23[row] * three,
                    c13[row] * one + c23[row] * two + c33[row] * three,
                ],
                axis=1,
            ).astype(jnp.bfloat16)
            mine = owner[slot]
            upper = mine > cross[mine]
            a = jnp.where(upper, left, solved)
            b = jnp.where(upper, solved, left)
            held[pl.ds(slot, PARAMS, stride=SLOTS + 1), :] = dot_nt(a, b)
        return carry

    lax.fori_loop(0, steps, body, 0)
    half = PARAMS // 2
    for col in range(PARAMS):
        lines = held[col * (SLOTS + 1) : col * (SLOTS + 1) + SLOTS, :]
        start = (col // half) * PARAMS * ROWS + col % half
        out[pl.ds(start, PARAMS, stride=ROWS), :] = lines.T


def sum_kernel(cross, arrived, out, hot, values, total, ranks):
    lines = lax.broadcasted_iota(jnp.int32, (PAIR_ORB, SLOTS), 0)
    total[...] = jnp.zeros_like(total)

    def body(step, carry):
        for i in range(STEP_SRC):
            base = (step * STEP_SRC + i) * ROWS
            piece = arrived[pl.ds(base, ELEMS), :]
            ids = arrived[pl.ds(base + ELEMS, 1), :].astype(jnp.int32)
            local = ids & (PAIR_ORB - 1)
            line = (ids >> 8) * 32 + (local >> 6) * 8 + (local & 7)
            group = (local >> 3) & 7
            at = slice(i * SLOTS, (i + 1) * SLOTS)
            hot[:, at] = jnp.where(lines == line, 1.0, 0.0).astype(jnp.bfloat16)
            for g in range(8):
                values[g * ELEMS : (g + 1) * ELEMS, at] = jnp.where(group == g, piece, 0.0).astype(jnp.bfloat16)
        total[...] += dot_nt(hot[...], values[...])
        return carry

    lax.fori_loop(0, DEVICES // STEP_SRC, body, 0)
    crossing_ranks(cross, ranks)
    for o in range(ORBITS):
        pair = pair_of(o, cross, ranks)
        for t in range(TILES):
            start = pl.multiple_of(pair * 32 + (t >> 1) * 8, 8)
            dest = (t * ORBITS + o) * 8
            out[dest : dest + 8, :] = total[pl.ds(start, 8), (t & 1) * 128 : (t & 1) * 128 + 128]


def place_kernel(cross, arrived, out, turned):
    me = lax.axis_index("orbit")
    upper = me > cross[me]
    lane = lax.broadcasted_iota(jnp.int32, (8, 128), 1)

    @pl.when(jnp.logical_not(upper))
    def _():
        band = lane // 32
        for tile in range(32):
            v = []
            for g in range(4):
                d = (g % 2) * PARAMS + 2 * tile + g // 2
                v.append(arrived[d * 8 : d * 8 + 8, :])
            moved = []
            for r in range(4):
                z = v[r]
                for h in range(1, 4):
                    z = jnp.where(band == h, v[(h + r) % 4], z)
                moved.append(z if r == 0 else pltpu.roll(z, 32 * r, 1))
            for h in range(4):
                u = moved[(0 - h) % 4]
                for g in range(1, 4):
                    u = jnp.where(band == g, moved[(g - h) % 4], u)
                start = (h * 32 + tile) * 8
                out[start : start + 8, :] = u

    @pl.when(upper)
    def _():
        low = lax.broadcasted_iota(jnp.int32, (64, 128), 1) < PARAMS
        for j in range(8):
            turned[...] = arrived[pl.ds(j, 128, stride=8), :].T
            even = turned[pl.ds(0, 64, stride=2), :]
            odd = turned[pl.ds(1, 64, stride=2), :]
            halves = (
                jnp.where(low, even, pltpu.roll(odd, PARAMS, 1)),
                jnp.where(low, pltpu.roll(even, PARAMS, 1), odd),
            )
            for h in range(4):
                for half in range(2):
                    start = h * 256 + half * 128 + j
                    out[pl.ds(start, 16, stride=8), :] = halves[half][h * 16 : h * 16 + 16]


def smem():
    return pl.BlockSpec(memory_space=pltpu.SMEM)


def exchange(x):
    return lax.all_to_all(x, ("tile", "orbit"), split_axis=0, concat_axis=0, tiled=True)


def in_vmem():
    return pl.BlockSpec(memory_space=pltpu.VMEM)


def in_hbm():
    return pl.BlockSpec(memory_space=pl.ANY)


def hbm(x):
    return pltpu.with_memory_space_constraint(x, pltpu.HBM)


def make_blocks(jacobians, point_normals, counts, owners, locals_, crossing):
    jac = jnp.transpose(jacobians, (0, 2, 1, 3)).reshape(SLOTS, 3 * PTS, 2 * PARAMS)
    normals = jnp.transpose(point_normals, (1, 0, 2))
    return pl.pallas_call(
        blocks_kernel,
        in_specs=[smem(), smem(), smem(), in_hbm(), in_hbm(), in_vmem(), in_vmem()],
        out_specs=in_vmem(),
        out_shape=pltpu.VMEM((DEVICES * ROWS, SLOTS), jnp.float32),
        scratch_shapes=[
            pltpu.VMEM((SLOTS, 3 * PTS, 2 * PARAMS), jnp.bfloat16),
            pltpu.VMEM((6, SLOTS, PTS), jnp.float32),
            pltpu.VMEM((PARAMS * (SLOTS + 1), PARAMS), jnp.float32),
            pltpu.SMEM((ORBITS,), jnp.int32),
            pltpu.SemaphoreType.DMA((SLOTS // STEP_SLOTS + 1,)),
        ],
        compiler_params=pltpu.CompilerParams(vmem_limit_bytes=24 << 20),
        name="blocks",
    )(*map(hbm, (counts, owners, crossing, jac, normals, owners.reshape(1, SLOTS), locals_.reshape(1, SLOTS))))


def sum_pairs(arrived, crossing):
    return pl.pallas_call(
        sum_kernel,
        in_specs=[smem(), in_vmem()],
        out_specs=in_vmem(),
        out_shape=pltpu.VMEM((DEVICES * 8, 128), jnp.float32),
        scratch_shapes=[
            pltpu.VMEM((PAIR_ORB, STEP_SRC * SLOTS), jnp.bfloat16),
            pltpu.VMEM((PAIR_ORB, STEP_SRC * SLOTS), jnp.bfloat16),
            pltpu.VMEM((PAIR_ORB, PAIR_ORB), jnp.float32),
            pltpu.SMEM((ORBITS,), jnp.int32),
        ],
        compiler_params=pltpu.CompilerParams(vmem_limit_bytes=12 << 20),
        name="sum_pairs",
    )(hbm(crossing), pltpu.with_memory_space_constraint(arrived, pltpu.VMEM))


def place(arrived, crossing):
    return pl.pallas_call(
        place_kernel,
        in_specs=[smem(), in_vmem()],
        out_specs=in_vmem(),
        out_shape=jax.ShapeDtypeStruct((DEVICES * 8, 128), jnp.float32),
        scratch_shapes=[pltpu.VMEM((128, 128), jnp.float32)],
        compiler_params=pltpu.CompilerParams(vmem_limit_bytes=8 << 20),
        name="place",
    )(hbm(crossing), pltpu.with_memory_space_constraint(arrived, pltpu.VMEM))


def local(jacobians, point_normals, block_counts, pair_owner, pair_local, crossing):
    sent = make_blocks(
        jacobians, point_normals, block_counts.reshape(SLOTS), pair_owner.reshape(SLOTS), pair_local, crossing
    )
    arrived = exchange(sent.reshape(DEVICES, ROWS, 1, SLOTS))
    sums = sum_pairs(arrived.reshape(DEVICES * ROWS, SLOTS), crossing)
    mine = exchange(sums.reshape(DEVICES, 8, 128))
    out = place(mine.reshape(DEVICES * 8, 128), crossing)
    out = jnp.transpose(out.reshape(4, 32, 8, 128), (0, 2, 1, 3))
    return out.reshape(1, PAIR_ORB // TILES, PARAMS * PARAMS)


def solution(mesh):
    both = ("tile", "orbit")
    in_specs = (
        P(both, None, None, None),
        P(both, None, None),
        P(both, None),
        P(both, None),
        P(both),
        P(),
    )
    return jax.shard_map(local, mesh=mesh, in_specs=in_specs, out_specs=P("orbit", "tile", None), check_vma=False)
```

```python
import jax
import jax.numpy as jnp
from jax import lax
from jax.experimental import pallas as pl
from jax.experimental.pallas import tpu as pltpu
from jax.sharding import PartitionSpec as P

DEVICES = 128
SLOTS = 128
PTS = 128
PARAMS = 64
ORBITS = 16
PAIR_ORB = 256
TILES = 8
ELEMS = PARAMS * PARAMS // DEVICES
ROWS = ELEMS + 1
STEP_SLOTS = 8
STEP_SRC = 64
NT = (((1,), (1,)), ((), ()))


def dot_nt(a, b):
    return lax.dot_general(a, b, NT, preferred_element_type=jnp.float32)


def eye(n):
    r = lax.broadcasted_iota(jnp.int32, (n, n), 0)
    c = lax.broadcasted_iota(jnp.int32, (n, n), 1)
    return jnp.where(r == c, 1.0, 0.0).astype(jnp.bfloat16)


def crossing_ranks(cross, ranks):
    seen = jnp.int32(0)
    for o in range(ORBITS):
        ranks[o] = seen
        seen = seen + (cross[o] > o).astype(jnp.int32)


def pair_of(o, cross, ranks):
    return ranks[jnp.minimum(o, cross[o])]


def blocks_kernel(counts, owner, cross, jac_hbm, normals_hbm, owner_row, local_row, out, jac, normals, held, planes, turned_a, turned_b, solved_a, solved_b, ranks, sems):
    steps = SLOTS // STEP_SLOTS
    copy_normals = pltpu.make_async_copy(normals_hbm, normals, sems.at[steps])
    copy_normals.start()

    def part(step):
        at = pl.ds(step * STEP_SLOTS, STEP_SLOTS)
        return pltpu.make_async_copy(jac_hbm.at[at], jac.at[at], sems.at[step])

    for step in range(steps):
        part(step).start()
    crossing_ranks(cross, ranks)
    names = owner_row[...]
    ids = jnp.zeros_like(names)
    for o in range(ORBITS):
        ids = jnp.where(names == o, pair_of(o, cross, ranks) * PAIR_ORB, ids)
    ids = (ids + local_row[...]).astype(jnp.float32)
    out[pl.ds(ELEMS, DEVICES, stride=ROWS), :] = jnp.broadcast_to(ids, (DEVICES, SLOTS))
    copy_normals.wait()
    sub = lax.broadcasted_iota(jnp.int32, (STEP_SLOTS, PTS), 0)
    place = lax.broadcasted_iota(jnp.int32, (STEP_SLOTS, PTS), 1)

    def turn(step, target):
        base = pl.multiple_of(step * STEP_SLOTS, STEP_SLOTS)
        for i in range(STEP_SLOTS):
            for q in range(3):
                target[i, q] = jac[base + i, q * PTS : (q + 1) * PTS, :].T

    def solve(step, source, target):
        base = pl.multiple_of(step * STEP_SLOTS, STEP_SLOTS)
        w11, w22, w33, w12, w13, w23 = (normals[q, pl.ds(base, STEP_SLOTS), :] for q in range(6))
        c11 = w22 * w33 - w23 * w23
        c22 = w11 * w33 - w13 * w13
        c33 = w11 * w22 - w12 * w12
        c12 = w13 * w23 - w12 * w33
        c13 = w12 * w23 - w13 * w22
        c23 = w12 * w13 - w11 * w23
        det = w11 * c11 + w12 * c12 + w13 * c13
        limit = jnp.zeros((STEP_SLOTS, PTS), jnp.int32)
        for i in range(STEP_SLOTS):
            limit = jnp.where(sub == i, counts[base + i], limit)
        weight = jnp.where(place < limit, 1.0, 0.0) / det
        c11, c22, c33 = c11 * weight, c22 * weight, c33 * weight
        c12, c13, c23 = c12 * weight, c13 * weight, c23 * weight
        for i in range(STEP_SLOTS):
            row = slice(i, i + 1)
            for first in range(0, PARAMS, 16):
                at = slice(first, first + 16)
                one, two, three = (source[i, q, PARAMS + first : PARAMS + first + 16, :].astype(jnp.float32) for q in range(3))
                target[i, 0, at, :] = (c11[row] * one + c12[row] * two + c13[row] * three).astype(jnp.bfloat16)
                target[i, 1, at, :] = (c12[row] * one + c22[row] * two + c23[row] * three).astype(jnp.bfloat16)
                target[i, 2, at, :] = (c13[row] * one + c23[row] * two + c33[row] * three).astype(jnp.bfloat16)
            block = dot_nt(jnp.concatenate([target[i, q] for q in range(3)], axis=1), jnp.concatenate([source[i, q, :PARAMS, :] for q in range(3)], axis=1))
            held[pl.ds(base + i, PARAMS, stride=SLOTS + 1), :] = block

    def body(pair, carry):
        step = pair * 2
        part(step + 1).wait()
        turn(step + 1, turned_b)
        solve(step, turned_a, solved_a)

        @pl.when(step + 2 < steps)
        def _():
            part(step + 2).wait()

        turn(jnp.minimum(step + 2, steps - 1), turned_a)
        solve(step + 1, turned_b, solved_b)
        return carry

    part(0).wait()
    turn(0, turned_a)
    lax.fori_loop(0, steps // 2, body, 0)
    for line in range(PARAMS):
        lines = held[line * (SLOTS + 1) : line * (SLOTS + 1) + SLOTS, :PARAMS].astype(jnp.bfloat16)
        planes[pl.ds(line, PARAMS, stride=PARAMS + 1), :] = lines.T.astype(jnp.float32)
    upper = jnp.zeros_like(names)
    for o in range(ORBITS):
        upper = jnp.where(names == o, (o > cross[o]).astype(jnp.int32), upper)
    upper = jnp.broadcast_to(upper, (PARAMS, SLOTS)) == 1
    half = PARAMS // 2
    for col in range(PARAMS):
        straight = planes[pl.ds(col, PARAMS, stride=PARAMS + 1), :]
        flipped = planes[col * (PARAMS + 1) : col * (PARAMS + 1) + PARAMS, :]
        start = (col // half) * PARAMS * ROWS + col % half
        out[pl.ds(start, PARAMS, stride=ROWS), :] = jnp.where(upper, flipped, straight)


def sum_kernel(cross, arrived, out, hot, values, total, ranks):
    lines = lax.broadcasted_iota(jnp.int32, (PAIR_ORB, SLOTS), 0).astype(jnp.bfloat16)
    one = jnp.ones((PAIR_ORB, SLOTS), jnp.bfloat16)
    none = jnp.zeros((PAIR_ORB, SLOTS), jnp.bfloat16)
    total[...] = jnp.zeros_like(total)

    def body(step, carry):
        for part in range(STEP_SRC // 64):
            hots, vals = [], []
            for i in range(64):
                base = (step * STEP_SRC + part * 64 + i) * ROWS
                piece = arrived[pl.ds(base, ELEMS), :].astype(jnp.bfloat16)
                ids = arrived[pl.ds(base + ELEMS, 1), :].astype(jnp.int32)
                local = ids & (PAIR_ORB - 1)
                line = ((ids >> 8) * 32 + (local >> 6) * 8 + (local & 7)).astype(jnp.bfloat16)
                group = jnp.broadcast_to(((local >> 3) & 7).astype(jnp.bfloat16), (ELEMS, SLOTS))
                hots.append(jnp.where(lines == line, one, none))
                vals.append(jnp.concatenate([jnp.where(group == g, piece, none[:ELEMS]) for g in range(8)], axis=0))
            total[...] += dot_nt(jnp.concatenate(hots, axis=1), jnp.concatenate(vals, axis=1))
        return carry

    lax.fori_loop(0, DEVICES // STEP_SRC, body, 0)
    crossing_ranks(cross, ranks)
    for o in range(ORBITS):
        pair = pair_of(o, cross, ranks)
        for t in range(TILES):
            start = pl.multiple_of(pair * 32 + (t >> 1) * 8, 8)
            dest = (t * ORBITS + o) * 8
            out[dest : dest + 8, :] = total[pl.ds(start, 8), (t & 1) * 128 : (t & 1) * 128 + 128]


def place_kernel(cross, arrived, out, turned):
    me = lax.axis_index("orbit")
    upper = me > cross[me]
    lane = lax.broadcasted_iota(jnp.int32, (8, 128), 1)

    @pl.when(jnp.logical_not(upper))
    def _():
        band = lane // 32
        for tile in range(32):
            v = []
            for g in range(4):
                d = (g % 2) * PARAMS + 2 * tile + g // 2
                v.append(arrived[d * 8 : d * 8 + 8, :])
            moved = []
            for r in range(4):
                z = v[r]
                for h in range(1, 4):
                    z = jnp.where(band == h, v[(h + r) % 4], z)
                moved.append(z if r == 0 else pltpu.roll(z, 32 * r, 1))
            for h in range(4):
                u = moved[(0 - h) % 4]
                for g in range(1, 4):
                    u = jnp.where(band == g, moved[(g - h) % 4], u)
                start = (h * 32 + tile) * 8
                out[start : start + 8, :] = u

    @pl.when(upper)
    def _():
        low = lax.broadcasted_iota(jnp.int32, (64, 128), 1) < PARAMS
        for j in range(8):
            turned[...] = arrived[pl.ds(j, 128, stride=8), :].T
            even = turned[pl.ds(0, 64, stride=2), :]
            odd = turned[pl.ds(1, 64, stride=2), :]
            halves = (
                jnp.where(low, even, pltpu.roll(odd, PARAMS, 1)),
                jnp.where(low, pltpu.roll(even, PARAMS, 1), odd),
            )
            for h in range(4):
                for half in range(2):
                    start = h * 256 + half * 128 + j
                    out[pl.ds(start, 16, stride=8), :] = halves[half][h * 16 : h * 16 + 16]


def smem():
    return pl.BlockSpec(memory_space=pltpu.SMEM)


def exchange(x):
    return lax.all_to_all(x, ("tile", "orbit"), split_axis=0, concat_axis=0, tiled=True)


def in_vmem():
    return pl.BlockSpec(memory_space=pltpu.VMEM)


def in_hbm():
    return pl.BlockSpec(memory_space=pl.ANY)


def hbm(x):
    return pltpu.with_memory_space_constraint(x, pltpu.HBM)


def make_blocks(jacobians, point_normals, counts, owners, locals_, crossing):
    jac = jnp.transpose(jacobians, (0, 2, 1, 3)).reshape(SLOTS, 3 * PTS, 2 * PARAMS)
    normals = jnp.transpose(point_normals, (1, 0, 2))
    return pl.pallas_call(
        blocks_kernel,
        in_specs=[smem(), smem(), smem(), in_hbm(), in_hbm(), in_vmem(), in_vmem()],
        out_specs=in_vmem(),
        out_shape=pltpu.VMEM((DEVICES * ROWS, SLOTS), jnp.float32),
        scratch_shapes=[
            pltpu.VMEM((SLOTS, 3 * PTS, 2 * PARAMS), jnp.bfloat16),
            pltpu.VMEM((6, SLOTS, PTS), jnp.float32),
            pltpu.VMEM((PARAMS * (SLOTS + 1), PARAMS), jnp.float32),
            pltpu.VMEM((PARAMS * (PARAMS + 1), SLOTS), jnp.float32),
            pltpu.VMEM((STEP_SLOTS, 3, 2 * PARAMS, PTS), jnp.bfloat16),
            pltpu.VMEM((STEP_SLOTS, 3, 2 * PARAMS, PTS), jnp.bfloat16),
            pltpu.VMEM((STEP_SLOTS, 3, PARAMS, PTS), jnp.bfloat16),
            pltpu.VMEM((STEP_SLOTS, 3, PARAMS, PTS), jnp.bfloat16),
            pltpu.SMEM((ORBITS,), jnp.int32),
            pltpu.SemaphoreType.DMA((SLOTS // STEP_SLOTS + 1,)),
        ],
        compiler_params=pltpu.CompilerParams(vmem_limit_bytes=24 << 20),
        name="blocks",
    )(*map(hbm, (counts, owners, crossing, jac, normals, owners.reshape(1, SLOTS), locals_.reshape(1, SLOTS))))


def sum_pairs(arrived, crossing):
    return pl.pallas_call(
        sum_kernel,
        in_specs=[smem(), in_vmem()],
        out_specs=in_vmem(),
        out_shape=pltpu.VMEM((DEVICES * 8, 128), jnp.float32),
        scratch_shapes=[
            pltpu.VMEM((PAIR_ORB, STEP_SRC * SLOTS), jnp.bfloat16),
            pltpu.VMEM((PAIR_ORB, STEP_SRC * SLOTS), jnp.bfloat16),
            pltpu.VMEM((PAIR_ORB, PAIR_ORB), jnp.float32),
            pltpu.SMEM((ORBITS,), jnp.int32),
        ],
        compiler_params=pltpu.CompilerParams(vmem_limit_bytes=24 << 20),
        name="sum_pairs",
    )(hbm(crossing), pltpu.with_memory_space_constraint(arrived, pltpu.VMEM))


def place(arrived, crossing):
    return pl.pallas_call(
        place_kernel,
        in_specs=[smem(), in_vmem()],
        out_specs=in_vmem(),
        out_shape=jax.ShapeDtypeStruct((DEVICES * 8, 128), jnp.float32),
        scratch_shapes=[pltpu.VMEM((128, 128), jnp.float32)],
        compiler_params=pltpu.CompilerParams(vmem_limit_bytes=8 << 20),
        name="place",
    )(hbm(crossing), pltpu.with_memory_space_constraint(arrived, pltpu.VMEM))


def local(jacobians, point_normals, block_counts, pair_owner, pair_local, crossing):
    sent = make_blocks(
        jacobians, point_normals, block_counts.reshape(SLOTS), pair_owner.reshape(SLOTS), pair_local, crossing
    )
    arrived = exchange(sent.reshape(DEVICES, ROWS, 1, SLOTS))
    sums = sum_pairs(arrived.reshape(DEVICES * ROWS, SLOTS), crossing)
    mine = exchange(sums.reshape(DEVICES, 8, 128))
    out = place(mine.reshape(DEVICES * 8, 128), crossing)
    out = jnp.transpose(out.reshape(4, 32, 8, 128), (0, 2, 1, 3))
    return out.reshape(1, PAIR_ORB // TILES, PARAMS * PARAMS)


def solution(mesh):
    both = ("tile", "orbit")
    in_specs = (
        P(both, None, None, None),
        P(both, None, None),
        P(both, None),
        P(both, None),
        P(both),
        P(),
    )
    return jax.shard_map(local, mesh=mesh, in_specs=in_specs, out_specs=P("orbit", "tile", None), check_vma=False)
```

```python
import jax
import jax.numpy as jnp
from jax import lax
from jax.experimental import pallas as pl
from jax.experimental.pallas import tpu as pltpu
from jax.sharding import PartitionSpec as P

DEVICES = 128
SLOTS = 128
PTS = 128
PARAMS = 64
ORBITS = 16
PAIR_ORB = 256
TILES = 8
ELEMS = PARAMS * PARAMS // DEVICES
ROWS = ELEMS + 1
STEP_SLOTS = 8
STEP_SRC = 128
NT = (((1,), (1,)), ((), ()))


def dot_nt(a, b):
    return lax.dot_general(a, b, NT, preferred_element_type=jnp.float32)


def eye(n):
    r = lax.broadcasted_iota(jnp.int32, (n, n), 0)
    c = lax.broadcasted_iota(jnp.int32, (n, n), 1)
    return jnp.where(r == c, 1.0, 0.0).astype(jnp.bfloat16)


def crossing_ranks(cross, ranks):
    seen = jnp.int32(0)
    for o in range(ORBITS):
        ranks[o] = seen
        seen = seen + (cross[o] > o).astype(jnp.int32)


def pair_of(o, cross, ranks):
    return ranks[jnp.minimum(o, cross[o])]


def blocks_kernel(counts, owner, cross, jac_hbm, normals_hbm, owner_row, local_row, out, jac, normals, held, planes, turned_a, turned_b, left_a, left_b, solved_a, solved_b, ranks, sems):
    steps = SLOTS // STEP_SLOTS
    copy_normals = pltpu.make_async_copy(normals_hbm, normals, sems.at[steps])
    copy_normals.start()

    def part(step):
        at = pl.ds(step * (2 * STEP_SLOTS), 2 * STEP_SLOTS)
        return pltpu.make_async_copy(jac_hbm.at[at], jac.at[at], sems.at[step])

    for step in range(steps // 2):
        part(step).start()
    crossing_ranks(cross, ranks)
    names = owner_row[...]
    ids = jnp.zeros_like(names)
    for o in range(ORBITS):
        ids = jnp.where(names == o, pair_of(o, cross, ranks) * PAIR_ORB, ids)
    ids = (ids + local_row[...]).astype(jnp.float32)
    out[pl.ds(ELEMS, DEVICES, stride=ROWS), :] = jnp.broadcast_to(ids, (DEVICES, SLOTS))
    copy_normals.wait()
    sub = lax.broadcasted_iota(jnp.int32, (STEP_SLOTS, PTS), 0)
    place = lax.broadcasted_iota(jnp.int32, (STEP_SLOTS, PTS), 1)

    def turn(step, target, left):
        base = pl.multiple_of(step * STEP_SLOTS, STEP_SLOTS)
        for i in range(STEP_SLOTS):
            for q in range(3):
                both = jac[base + i, q * PTS : (q + 1) * PTS, :].T
                target[i, q] = both[PARAMS:].astype(jnp.float32)
                left[i, q] = both[:PARAMS]

    def solve(step, source, left, target):
        base = pl.multiple_of(step * STEP_SLOTS, STEP_SLOTS)
        w11, w22, w33, w12, w13, w23 = (normals[q, pl.ds(base, STEP_SLOTS), :] for q in range(6))
        c11 = w22 * w33 - w23 * w23
        c22 = w11 * w33 - w13 * w13
        c33 = w11 * w22 - w12 * w12
        c12 = w13 * w23 - w12 * w33
        c13 = w12 * w23 - w13 * w22
        c23 = w12 * w13 - w11 * w23
        det = w11 * c11 + w12 * c12 + w13 * c13
        limit = jnp.zeros((STEP_SLOTS, PTS), jnp.int32)
        for i in range(STEP_SLOTS):
            limit = jnp.where(sub == i, counts[base + i], limit)
        weight = jnp.where(place < limit, 1.0, 0.0) / det
        c11, c22, c33 = c11 * weight, c22 * weight, c33 * weight
        c12, c13, c23 = c12 * weight, c13 * weight, c23 * weight
        for i in range(STEP_SLOTS):
            row = slice(i, i + 1)
            for first in range(0, PARAMS, 16):
                at = slice(first, first + 16)
                one, two, three = (source[i, q, at, :] for q in range(3))
                target[i, 0, at, :] = (c11[row] * one + c12[row] * two + c13[row] * three).astype(jnp.bfloat16)
                target[i, 1, at, :] = (c12[row] * one + c22[row] * two + c23[row] * three).astype(jnp.bfloat16)
                target[i, 2, at, :] = (c13[row] * one + c23[row] * two + c33[row] * three).astype(jnp.bfloat16)
            block = dot_nt(jnp.concatenate([target[i, q] for q in range(3)], axis=1), jnp.concatenate([left[i, q] for q in range(3)], axis=1))
            held[pl.ds(base + i, PARAMS, stride=SLOTS + 1), :] = block

    def body(pair, carry):
        step = pair * 2
        part(pair).wait()
        turn(step, turned_a, left_a)
        solve(jnp.maximum(step - 1, 0), turned_b, left_b, solved_b)
        turn(step + 1, turned_b, left_b)
        solve(step, turned_a, left_a, solved_a)
        return carry

    turned_b[...] = jnp.zeros_like(turned_b)
    left_b[...] = jnp.zeros_like(left_b)
    lax.fori_loop(0, steps // 2, body, 0)
    solve(steps - 1, turned_b, left_b, solved_b)
    for line in range(PARAMS):
        lines = held[line * (SLOTS + 1) : line * (SLOTS + 1) + SLOTS, :PARAMS].astype(jnp.bfloat16)
        planes[pl.ds(line, PARAMS, stride=PARAMS + 1), :] = lines.T.astype(jnp.float32)
    upper = jnp.zeros_like(names)
    for o in range(ORBITS):
        upper = jnp.where(names == o, (o > cross[o]).astype(jnp.int32), upper)
    upper = jnp.broadcast_to(upper, (PARAMS, SLOTS)) == 1
    half = PARAMS // 2
    for col in range(PARAMS):
        straight = planes[pl.ds(col, PARAMS, stride=PARAMS + 1), :]
        flipped = planes[col * (PARAMS + 1) : col * (PARAMS + 1) + PARAMS, :]
        start = (col // half) * PARAMS * ROWS + col % half
        out[pl.ds(start, PARAMS, stride=ROWS), :] = jnp.where(upper, flipped, straight)


def sum_kernel(cross, arrived, out, hot, values, total, ranks):
    lines = lax.broadcasted_iota(jnp.int32, (PAIR_ORB, SLOTS), 0).astype(jnp.bfloat16)
    one = jnp.ones((PAIR_ORB, SLOTS), jnp.bfloat16)
    none = jnp.zeros((PAIR_ORB, SLOTS), jnp.bfloat16)
    total[...] = jnp.zeros_like(total)

    def body(step, carry):
        for part in range(STEP_SRC // 128):
            hots, vals = [], []
            for i in range(128):
                base = (step * STEP_SRC + part * 128 + i) * ROWS
                piece = arrived[pl.ds(base, ELEMS), :].astype(jnp.bfloat16)
                ids = arrived[pl.ds(base + ELEMS, 1), :].astype(jnp.int32)
                local = ids & (PAIR_ORB - 1)
                line = ((ids >> 8) * 32 + (local >> 6) * 8 + (local & 7)).astype(jnp.bfloat16)
                group = jnp.broadcast_to(((local >> 3) & 7).astype(jnp.bfloat16), (ELEMS, SLOTS))
                hots.append(jnp.where(lines == line, one, none))
                vals.append(jnp.concatenate([jnp.where(group == g, piece, none[:ELEMS]) for g in range(8)], axis=0))
            total[...] += dot_nt(jnp.concatenate(hots, axis=1), jnp.concatenate(vals, axis=1))
        return carry

    lax.fori_loop(0, DEVICES // STEP_SRC, body, 0)
    crossing_ranks(cross, ranks)
    for o in range(ORBITS):
        pair = pair_of(o, cross, ranks)
        for t in range(TILES):
            start = pl.multiple_of(pair * 32 + (t >> 1) * 8, 8)
            dest = (t * ORBITS + o) * 8
            out[dest : dest + 8, :] = total[pl.ds(start, 8), (t & 1) * 128 : (t & 1) * 128 + 128]


def place_kernel(cross, arrived, out, turned):
    me = lax.axis_index("orbit")
    upper = me > cross[me]
    lane = lax.broadcasted_iota(jnp.int32, (8, 128), 1)

    @pl.when(jnp.logical_not(upper))
    def _():
        band = lane // 32
        for tile in range(32):
            v = []
            for g in range(4):
                d = (g % 2) * PARAMS + 2 * tile + g // 2
                v.append(arrived[d * 8 : d * 8 + 8, :])
            moved = []
            for r in range(4):
                z = v[r]
                for h in range(1, 4):
                    z = jnp.where(band == h, v[(h + r) % 4], z)
                moved.append(z if r == 0 else pltpu.roll(z, 32 * r, 1))
            for h in range(4):
                u = moved[(0 - h) % 4]
                for g in range(1, 4):
                    u = jnp.where(band == g, moved[(g - h) % 4], u)
                start = (h * 32 + tile) * 8
                out[start : start + 8, :] = u

    @pl.when(upper)
    def _():
        low = lax.broadcasted_iota(jnp.int32, (64, 128), 1) < PARAMS
        for j in range(8):
            turned[...] = arrived[pl.ds(j, 128, stride=8), :].T
            even = turned[pl.ds(0, 64, stride=2), :]
            odd = turned[pl.ds(1, 64, stride=2), :]
            halves = (
                jnp.where(low, even, pltpu.roll(odd, PARAMS, 1)),
                jnp.where(low, pltpu.roll(even, PARAMS, 1), odd),
            )
            for h in range(4):
                for half in range(2):
                    start = h * 256 + half * 128 + j
                    out[pl.ds(start, 16, stride=8), :] = halves[half][h * 16 : h * 16 + 16]


def smem():
    return pl.BlockSpec(memory_space=pltpu.SMEM)


def exchange(x):
    return lax.all_to_all(x, ("tile", "orbit"), split_axis=0, concat_axis=0, tiled=True)


def in_vmem():
    return pl.BlockSpec(memory_space=pltpu.VMEM)


def in_hbm():
    return pl.BlockSpec(memory_space=pl.ANY)


def hbm(x):
    return pltpu.with_memory_space_constraint(x, pltpu.HBM)


def make_blocks(jacobians, point_normals, counts, owners, locals_, crossing):
    jac = jnp.transpose(jacobians, (0, 2, 1, 3)).reshape(SLOTS, 3 * PTS, 2 * PARAMS)
    normals = jnp.transpose(point_normals, (1, 0, 2))
    return pl.pallas_call(
        blocks_kernel,
        in_specs=[smem(), smem(), smem(), in_hbm(), in_hbm(), in_vmem(), in_vmem()],
        out_specs=in_vmem(),
        out_shape=pltpu.VMEM((DEVICES * ROWS, SLOTS), jnp.float32),
        scratch_shapes=[
            pltpu.VMEM((SLOTS, 3 * PTS, 2 * PARAMS), jnp.bfloat16),
            pltpu.VMEM((6, SLOTS, PTS), jnp.float32),
            pltpu.VMEM((PARAMS * (SLOTS + 1), PARAMS), jnp.float32),
            pltpu.VMEM((PARAMS * (PARAMS + 1), SLOTS), jnp.float32),
            pltpu.VMEM((STEP_SLOTS, 3, PARAMS, PTS), jnp.float32),
            pltpu.VMEM((STEP_SLOTS, 3, PARAMS, PTS), jnp.float32),
            pltpu.VMEM((STEP_SLOTS, 3, PARAMS, PTS), jnp.bfloat16),
            pltpu.VMEM((STEP_SLOTS, 3, PARAMS, PTS), jnp.bfloat16),
            pltpu.VMEM((STEP_SLOTS, 3, PARAMS, PTS), jnp.bfloat16),
            pltpu.VMEM((STEP_SLOTS, 3, PARAMS, PTS), jnp.bfloat16),
            pltpu.SMEM((ORBITS,), jnp.int32),
            pltpu.SemaphoreType.DMA((SLOTS // STEP_SLOTS + 1,)),
        ],
        compiler_params=pltpu.CompilerParams(vmem_limit_bytes=28 << 20),
        name="blocks",
    )(*map(hbm, (counts, owners, crossing, jac, normals, owners.reshape(1, SLOTS), locals_.reshape(1, SLOTS))))


def sum_pairs(arrived, crossing):
    return pl.pallas_call(
        sum_kernel,
        in_specs=[smem(), in_vmem()],
        out_specs=in_vmem(),
        out_shape=pltpu.VMEM((DEVICES * 8, 128), jnp.float32),
        scratch_shapes=[
            pltpu.VMEM((PAIR_ORB, STEP_SRC * SLOTS), jnp.bfloat16),
            pltpu.VMEM((PAIR_ORB, STEP_SRC * SLOTS), jnp.bfloat16),
            pltpu.VMEM((PAIR_ORB, PAIR_ORB), jnp.float32),
            pltpu.SMEM((ORBITS,), jnp.int32),
        ],
        compiler_params=pltpu.CompilerParams(vmem_limit_bytes=28 << 20),
        name="sum_pairs",
    )(hbm(crossing), pltpu.with_memory_space_constraint(arrived, pltpu.VMEM))


def place(arrived, crossing):
    return pl.pallas_call(
        place_kernel,
        in_specs=[smem(), in_vmem()],
        out_specs=in_vmem(),
        out_shape=jax.ShapeDtypeStruct((DEVICES * 8, 128), jnp.float32),
        scratch_shapes=[pltpu.VMEM((128, 128), jnp.float32)],
        compiler_params=pltpu.CompilerParams(vmem_limit_bytes=8 << 20),
        name="place",
    )(hbm(crossing), pltpu.with_memory_space_constraint(arrived, pltpu.VMEM))


def local(jacobians, point_normals, block_counts, pair_owner, pair_local, crossing):
    sent = make_blocks(
        jacobians, point_normals, block_counts.reshape(SLOTS), pair_owner.reshape(SLOTS), pair_local, crossing
    )
    arrived = exchange(sent.reshape(DEVICES, ROWS, 1, SLOTS))
    sums = sum_pairs(arrived.reshape(DEVICES * ROWS, SLOTS), crossing)
    mine = exchange(sums.reshape(DEVICES, 8, 128))
    out = place(mine.reshape(DEVICES * 8, 128), crossing)
    out = jnp.transpose(out.reshape(4, 32, 8, 128), (0, 2, 1, 3))
    return out.reshape(1, PAIR_ORB // TILES, PARAMS * PARAMS)


def solution(mesh):
    both = ("tile", "orbit")
    in_specs = (
        P(both, None, None, None),
        P(both, None, None),
        P(both, None),
        P(both, None),
        P(both),
        P(),
    )
    return jax.shard_map(local, mesh=mesh, in_specs=in_specs, out_specs=P("orbit", "tile", None), check_vma=False)
```

```python
import jax
import jax.numpy as jnp
from jax import lax
from jax.experimental import pallas as pl
from jax.experimental.pallas import tpu as pltpu
from jax.sharding import PartitionSpec as P

DEVICES = 128
SLOTS = 128
PTS = 128
PARAMS = 64
ORBITS = 16
PAIR_ORB = 256
TILES = 8
ELEMS = PARAMS * PARAMS // DEVICES
ROWS = ELEMS + 1
STEP_SLOTS = 8
STEP_SRC = 128
NT = (((1,), (1,)), ((), ()))


def dot_nt(a, b):
    return lax.dot_general(a, b, NT, preferred_element_type=jnp.float32)


def eye(n):
    r = lax.broadcasted_iota(jnp.int32, (n, n), 0)
    c = lax.broadcasted_iota(jnp.int32, (n, n), 1)
    return jnp.where(r == c, 1.0, 0.0).astype(jnp.bfloat16)


def crossing_ranks(cross, ranks):
    seen = jnp.int32(0)
    for o in range(ORBITS):
        ranks[o] = seen
        seen = seen + (cross[o] > o).astype(jnp.int32)


def pair_of(o, cross, ranks):
    return ranks[jnp.minimum(o, cross[o])]


def blocks_kernel(counts, owner, cross, jac_hbm, normals_hbm, owner_row, local_row, out, jac, normals, held, planes, turned_a, turned_b, left_a, left_b, solved_a, solved_b, ranks, sems):
    steps = SLOTS // STEP_SLOTS
    copy_normals = pltpu.make_async_copy(normals_hbm, normals, sems.at[steps])
    copy_normals.start()

    def part(step):
        at = pl.ds(step * (2 * STEP_SLOTS), 2 * STEP_SLOTS)
        return pltpu.make_async_copy(jac_hbm.at[at], jac.at[at], sems.at[step])

    for step in range(steps // 2):
        part(step).start()
    crossing_ranks(cross, ranks)
    names = owner_row[...]
    ids = jnp.zeros_like(names)
    for o in range(ORBITS):
        ids = jnp.where(names == o, pair_of(o, cross, ranks) * PAIR_ORB, ids)
    ids = (ids + local_row[...]).astype(jnp.float32)
    out[pl.ds(ELEMS, DEVICES, stride=ROWS), :] = jnp.broadcast_to(ids, (DEVICES, SLOTS))
    copy_normals.wait()
    ident = eye(2 * PARAMS)
    sub = lax.broadcasted_iota(jnp.int32, (STEP_SLOTS, PTS), 0)
    place = lax.broadcasted_iota(jnp.int32, (STEP_SLOTS, PTS), 1)

    def turn(step, target, left, late):
        base = pl.multiple_of(step * STEP_SLOTS, STEP_SLOTS)
        for i in range(STEP_SLOTS):
            for q in range(3):
                piece = jac[base + i, q * PTS : (q + 1) * PTS, :]
                both = dot_nt(ident, piece) if late and i >= 6 else piece.T
                target[i, q] = both[PARAMS:].astype(jnp.float32)
                left[i, q] = both[:PARAMS].astype(jnp.bfloat16)

    def solve(step, source, left, target):
        base = pl.multiple_of(step * STEP_SLOTS, STEP_SLOTS)
        w11, w22, w33, w12, w13, w23 = (normals[q, pl.ds(base, STEP_SLOTS), :] for q in range(6))
        c11 = w22 * w33 - w23 * w23
        c22 = w11 * w33 - w13 * w13
        c33 = w11 * w22 - w12 * w12
        c12 = w13 * w23 - w12 * w33
        c13 = w12 * w23 - w13 * w22
        c23 = w12 * w13 - w11 * w23
        det = w11 * c11 + w12 * c12 + w13 * c13
        limit = jnp.zeros((STEP_SLOTS, PTS), jnp.int32)
        for i in range(STEP_SLOTS):
            limit = jnp.where(sub == i, counts[base + i], limit)
        weight = jnp.where(place < limit, 1.0, 0.0) / det
        c11, c22, c33 = c11 * weight, c22 * weight, c33 * weight
        c12, c13, c23 = c12 * weight, c13 * weight, c23 * weight
        for i in range(STEP_SLOTS):
            row = slice(i, i + 1)
            for first in range(0, PARAMS, 16):
                at = slice(first, first + 16)
                one, two, three = (source[i, q, at, :] for q in range(3))
                target[i, 0, at, :] = (c11[row] * one + c12[row] * two + c13[row] * three).astype(jnp.bfloat16)
                target[i, 1, at, :] = (c12[row] * one + c22[row] * two + c23[row] * three).astype(jnp.bfloat16)
                target[i, 2, at, :] = (c13[row] * one + c23[row] * two + c33[row] * three).astype(jnp.bfloat16)
            block = dot_nt(jnp.concatenate([target[i, q] for q in range(3)], axis=1), jnp.concatenate([left[i, q] for q in range(3)], axis=1))
            held[pl.ds(base + i, PARAMS, stride=SLOTS + 1), :] = block

    def body(pair, carry):
        step = pair * 2
        part(pair).wait()
        turn(step, turned_a, left_a, False)
        solve(jnp.maximum(step - 1, 0), turned_b, left_b, solved_b)
        turn(step + 1, turned_b, left_b, True)
        solve(step, turned_a, left_a, solved_a)
        return carry

    turned_b[...] = jnp.zeros_like(turned_b)
    left_b[...] = jnp.zeros_like(left_b)
    lax.fori_loop(0, steps // 2, body, 0)
    solve(steps - 1, turned_b, left_b, solved_b)
    for line in range(PARAMS):
        lines = held[line * (SLOTS + 1) : line * (SLOTS + 1) + SLOTS, :PARAMS].astype(jnp.bfloat16)
        planes[pl.ds(line, PARAMS, stride=PARAMS + 1), :] = lines.T.astype(jnp.float32)
    upper = jnp.zeros_like(names)
    for o in range(ORBITS):
        upper = jnp.where(names == o, (o > cross[o]).astype(jnp.int32), upper)
    upper = jnp.broadcast_to(upper, (PARAMS, SLOTS)) == 1
    half = PARAMS // 2
    for col in range(PARAMS):
        straight = planes[pl.ds(col, PARAMS, stride=PARAMS + 1), :]
        flipped = planes[col * (PARAMS + 1) : col * (PARAMS + 1) + PARAMS, :]
        start = (col // half) * PARAMS * ROWS + col % half
        out[pl.ds(start, PARAMS, stride=ROWS), :] = jnp.where(upper, flipped, straight)


def sum_kernel(cross, arrived, out, hot, values, total, ranks):
    lines = lax.broadcasted_iota(jnp.int32, (PAIR_ORB, SLOTS), 0).astype(jnp.bfloat16)
    one = jnp.ones((PAIR_ORB, SLOTS), jnp.bfloat16)
    none = jnp.zeros((PAIR_ORB, SLOTS), jnp.bfloat16)
    total[...] = jnp.zeros_like(total)

    def body(step, carry):
        for part in range(STEP_SRC // 128):
            hots, vals = [], []
            for i in range(128):
                base = (step * STEP_SRC + part * 128 + i) * ROWS
                piece = arrived[pl.ds(base, ELEMS), :].astype(jnp.bfloat16)
                ids = arrived[pl.ds(base + ELEMS, 1), :].astype(jnp.int32)
                local = ids & (PAIR_ORB - 1)
                line = ((ids >> 8) * 32 + (local >> 6) * 8 + (local & 7)).astype(jnp.bfloat16)
                group = jnp.broadcast_to(((local >> 3) & 7).astype(jnp.bfloat16), (ELEMS, SLOTS))
                hots.append(jnp.where(lines == line, one, none))
                vals.append(jnp.concatenate([jnp.where(group == g, piece, none[:ELEMS]) for g in range(8)], axis=0))
            total[...] += dot_nt(jnp.concatenate(hots, axis=1), jnp.concatenate(vals, axis=1))
        return carry

    lax.fori_loop(0, DEVICES // STEP_SRC, body, 0)
    crossing_ranks(cross, ranks)
    for o in range(ORBITS):
        pair = pair_of(o, cross, ranks)
        for t in range(TILES):
            start = pl.multiple_of(pair * 32 + (t >> 1) * 8, 8)
            dest = (t * ORBITS + o) * 8
            out[dest : dest + 8, :] = total[pl.ds(start, 8), (t & 1) * 128 : (t & 1) * 128 + 128]


def place_kernel(cross, arrived, out, turned):
    me = lax.axis_index("orbit")
    upper = me > cross[me]
    lane = lax.broadcasted_iota(jnp.int32, (8, 128), 1)

    @pl.when(jnp.logical_not(upper))
    def _():
        band = lane // 32
        for tile in range(32):
            v = []
            for g in range(4):
                d = (g % 2) * PARAMS + 2 * tile + g // 2
                v.append(arrived[d * 8 : d * 8 + 8, :])
            moved = []
            for r in range(4):
                z = v[r]
                for h in range(1, 4):
                    z = jnp.where(band == h, v[(h + r) % 4], z)
                moved.append(z if r == 0 else pltpu.roll(z, 32 * r, 1))
            for h in range(4):
                u = moved[(0 - h) % 4]
                for g in range(1, 4):
                    u = jnp.where(band == g, moved[(g - h) % 4], u)
                start = (h * 32 + tile) * 8
                out[start : start + 8, :] = u

    @pl.when(upper)
    def _():
        low = lax.broadcasted_iota(jnp.int32, (64, 128), 1) < PARAMS
        for j in range(8):
            turned[...] = arrived[pl.ds(j, 128, stride=8), :].T
            even = turned[pl.ds(0, 64, stride=2), :]
            odd = turned[pl.ds(1, 64, stride=2), :]
            halves = (
                jnp.where(low, even, pltpu.roll(odd, PARAMS, 1)),
                jnp.where(low, pltpu.roll(even, PARAMS, 1), odd),
            )
            for h in range(4):
                for half in range(2):
                    start = h * 256 + half * 128 + j
                    out[pl.ds(start, 16, stride=8), :] = halves[half][h * 16 : h * 16 + 16]


def smem():
    return pl.BlockSpec(memory_space=pltpu.SMEM)


def exchange(x):
    return lax.all_to_all(x, ("tile", "orbit"), split_axis=0, concat_axis=0, tiled=True)


def in_vmem():
    return pl.BlockSpec(memory_space=pltpu.VMEM)


def in_hbm():
    return pl.BlockSpec(memory_space=pl.ANY)


def hbm(x):
    return pltpu.with_memory_space_constraint(x, pltpu.HBM)


def make_blocks(jacobians, point_normals, counts, owners, locals_, crossing):
    jac = jnp.transpose(jacobians, (0, 2, 1, 3)).reshape(SLOTS, 3 * PTS, 2 * PARAMS)
    normals = jnp.transpose(point_normals, (1, 0, 2))
    return pl.pallas_call(
        blocks_kernel,
        in_specs=[smem(), smem(), smem(), in_hbm(), in_hbm(), in_vmem(), in_vmem()],
        out_specs=in_vmem(),
        out_shape=pltpu.VMEM((DEVICES * ROWS, SLOTS), jnp.float32),
        scratch_shapes=[
            pltpu.VMEM((SLOTS, 3 * PTS, 2 * PARAMS), jnp.bfloat16),
            pltpu.VMEM((6, SLOTS, PTS), jnp.float32),
            pltpu.VMEM((PARAMS * (SLOTS + 1), PARAMS), jnp.float32),
            pltpu.VMEM((PARAMS * (PARAMS + 1), SLOTS), jnp.float32),
            pltpu.VMEM((STEP_SLOTS, 3, PARAMS, PTS), jnp.float32),
            pltpu.VMEM((STEP_SLOTS, 3, PARAMS, PTS), jnp.float32),
            pltpu.VMEM((STEP_SLOTS, 3, PARAMS, PTS), jnp.bfloat16),
            pltpu.VMEM((STEP_SLOTS, 3, PARAMS, PTS), jnp.bfloat16),
            pltpu.VMEM((STEP_SLOTS, 3, PARAMS, PTS), jnp.bfloat16),
            pltpu.VMEM((STEP_SLOTS, 3, PARAMS, PTS), jnp.bfloat16),
            pltpu.SMEM((ORBITS,), jnp.int32),
            pltpu.SemaphoreType.DMA((SLOTS // STEP_SLOTS + 1,)),
        ],
        compiler_params=pltpu.CompilerParams(vmem_limit_bytes=28 << 20),
        name="blocks",
    )(*map(hbm, (counts, owners, crossing, jac, normals, owners.reshape(1, SLOTS), locals_.reshape(1, SLOTS))))


def sum_pairs(arrived, crossing):
    return pl.pallas_call(
        sum_kernel,
        in_specs=[smem(), in_vmem()],
        out_specs=in_vmem(),
        out_shape=pltpu.VMEM((DEVICES * 8, 128), jnp.float32),
        scratch_shapes=[
            pltpu.VMEM((PAIR_ORB, STEP_SRC * SLOTS), jnp.bfloat16),
            pltpu.VMEM((PAIR_ORB, STEP_SRC * SLOTS), jnp.bfloat16),
            pltpu.VMEM((PAIR_ORB, PAIR_ORB), jnp.float32),
            pltpu.SMEM((ORBITS,), jnp.int32),
        ],
        compiler_params=pltpu.CompilerParams(vmem_limit_bytes=28 << 20),
        name="sum_pairs",
    )(hbm(crossing), pltpu.with_memory_space_constraint(arrived, pltpu.VMEM))


def place(arrived, crossing):
    return pl.pallas_call(
        place_kernel,
        in_specs=[smem(), in_vmem()],
        out_specs=in_vmem(),
        out_shape=jax.ShapeDtypeStruct((DEVICES * 8, 128), jnp.float32),
        scratch_shapes=[pltpu.VMEM((128, 128), jnp.float32)],
        compiler_params=pltpu.CompilerParams(vmem_limit_bytes=8 << 20),
        name="place",
    )(hbm(crossing), pltpu.with_memory_space_constraint(arrived, pltpu.VMEM))


def local(jacobians, point_normals, block_counts, pair_owner, pair_local, crossing):
    sent = make_blocks(
        jacobians, point_normals, block_counts.reshape(SLOTS), pair_owner.reshape(SLOTS), pair_local, crossing
    )
    arrived = exchange(sent.reshape(DEVICES, ROWS, 1, SLOTS))
    sums = sum_pairs(arrived.reshape(DEVICES * ROWS, SLOTS), crossing)
    mine = exchange(sums.reshape(DEVICES, 8, 128))
    out = place(mine.reshape(DEVICES * 8, 128), crossing)
    out = jnp.transpose(out.reshape(4, 32, 8, 128), (0, 2, 1, 3))
    return out.reshape(1, PAIR_ORB // TILES, PARAMS * PARAMS)


def solution(mesh):
    both = ("tile", "orbit")
    in_specs = (
        P(both, None, None, None),
        P(both, None, None),
        P(both, None),
        P(both, None),
        P(both),
        P(),
    )
    return jax.shard_map(local, mesh=mesh, in_specs=in_specs, out_specs=P("orbit", "tile", None), check_vma=False)
```

```python
import jax
import jax.numpy as jnp
from jax import lax
from jax.experimental import pallas as pl
from jax.experimental.pallas import tpu as pltpu
from jax.sharding import PartitionSpec as P

DEVICES = 128
SLOTS = 128
PTS = 128
PARAMS = 64
ORBITS = 16
PAIR_ORB = 256
TILES = 8
ELEMS = PARAMS * PARAMS // DEVICES
ROWS = ELEMS + 1
STEP_SLOTS = 8
STEP_SRC = 128
NT = (((1,), (1,)), ((), ()))


def dot_nt(a, b):
    return lax.dot_general(a, b, NT, preferred_element_type=jnp.float32)


def eye(n):
    r = lax.broadcasted_iota(jnp.int32, (n, n), 0)
    c = lax.broadcasted_iota(jnp.int32, (n, n), 1)
    return jnp.where(r == c, 1.0, 0.0).astype(jnp.bfloat16)


def crossing_ranks(cross, ranks):
    seen = jnp.int32(0)
    for o in range(ORBITS):
        ranks[o] = seen
        seen = seen + (cross[o] > o).astype(jnp.int32)


def pair_of(o, cross, ranks):
    return ranks[jnp.minimum(o, cross[o])]


def blocks_kernel(counts, owner, cross, jac_hbm, normals_hbm, owner_row, local_row, out, jac, normals, held, planes, turned_a, turned_b, left_a, left_b, solved_a, solved_b, ranks, sems):
    steps = SLOTS // STEP_SLOTS
    copy_normals = pltpu.make_async_copy(normals_hbm, normals, sems.at[steps])
    copy_normals.start()

    def part(step):
        at = pl.ds(step * (2 * STEP_SLOTS), 2 * STEP_SLOTS)
        return pltpu.make_async_copy(jac_hbm.at[at], jac.at[at], sems.at[step])

    for step in range(steps // 2):
        part(step).start()
    crossing_ranks(cross, ranks)
    names = owner_row[...]
    ids = jnp.zeros_like(names)
    for o in range(ORBITS):
        ids = jnp.where(names == o, pair_of(o, cross, ranks) * PAIR_ORB, ids)
    ids = (ids + local_row[...]).astype(jnp.float32)
    out[pl.ds(ELEMS, DEVICES, stride=ROWS), :] = jnp.broadcast_to(ids, (DEVICES, SLOTS))
    copy_normals.wait()
    ident = eye(2 * PARAMS)
    sub = lax.broadcasted_iota(jnp.int32, (STEP_SLOTS, PTS), 0)
    place = lax.broadcasted_iota(jnp.int32, (STEP_SLOTS, PTS), 1)

    def turn(step, target, left, late):
        base = pl.multiple_of(step * STEP_SLOTS, STEP_SLOTS)
        for i in range(STEP_SLOTS):
            for q in range(3):
                piece = jac[base + i, q * PTS : (q + 1) * PTS, :]
                both = dot_nt(ident, piece) if late and (i >= 6 or (i == 5 and q == 2)) else piece.T
                target[i, q] = both[PARAMS:].astype(jnp.float32)
                left[i, q] = both[:PARAMS].astype(jnp.bfloat16)

    def solve(step, source, left, target):
        base = pl.multiple_of(step * STEP_SLOTS, STEP_SLOTS)
        w11, w22, w33, w12, w13, w23 = (normals[q, pl.ds(base, STEP_SLOTS), :] for q in range(6))
        c11 = w22 * w33 - w23 * w23
        c22 = w11 * w33 - w13 * w13
        c33 = w11 * w22 - w12 * w12
        c12 = w13 * w23 - w12 * w33
        c13 = w12 * w23 - w13 * w22
        c23 = w12 * w13 - w11 * w23
        det = w11 * c11 + w12 * c12 + w13 * c13
        limit = jnp.zeros((STEP_SLOTS, PTS), jnp.int32)
        for i in range(STEP_SLOTS):
            limit = jnp.where(sub == i, counts[base + i], limit)
        weight = jnp.where(place < limit, 1.0, 0.0) / det
        c11, c22, c33 = c11 * weight, c22 * weight, c33 * weight
        c12, c13, c23 = c12 * weight, c13 * weight, c23 * weight
        for i in range(STEP_SLOTS):
            row = slice(i, i + 1)
            for first in range(0, PARAMS, 16):
                at = slice(first, first + 16)
                one, two, three = (source[i, q, at, :] for q in range(3))
                target[i, 0, at, :] = (c11[row] * one + c12[row] * two + c13[row] * three).astype(jnp.bfloat16)
                target[i, 1, at, :] = (c12[row] * one + c22[row] * two + c23[row] * three).astype(jnp.bfloat16)
                target[i, 2, at, :] = (c13[row] * one + c23[row] * two + c33[row] * three).astype(jnp.bfloat16)
            block = dot_nt(jnp.concatenate([target[i, q] for q in range(3)], axis=1), jnp.concatenate([left[i, q] for q in range(3)], axis=1))
            held[pl.ds(base + i, PARAMS, stride=SLOTS + 1), :] = block

    def body(pair, carry):
        step = pair * 2
        part(pair).wait()
        turn(step, turned_a, left_a, False)
        solve(jnp.maximum(step - 1, 0), turned_b, left_b, solved_b)
        turn(step + 1, turned_b, left_b, True)
        solve(step, turned_a, left_a, solved_a)
        return carry

    turned_b[...] = jnp.zeros_like(turned_b)
    left_b[...] = jnp.zeros_like(left_b)
    lax.fori_loop(0, steps // 2, body, 0)
    solve(steps - 1, turned_b, left_b, solved_b)
    for line in range(PARAMS):
        lines = held[line * (SLOTS + 1) : line * (SLOTS + 1) + SLOTS, :PARAMS].astype(jnp.bfloat16)
        planes[pl.ds(line, PARAMS, stride=PARAMS + 1), :] = lines.T.astype(jnp.float32)
    upper = jnp.zeros_like(names)
    for o in range(ORBITS):
        upper = jnp.where(names == o, (o > cross[o]).astype(jnp.int32), upper)
    upper = jnp.broadcast_to(upper, (PARAMS, SLOTS)) == 1
    half = PARAMS // 2
    for col in range(PARAMS):
        straight = planes[pl.ds(col, PARAMS, stride=PARAMS + 1), :]
        flipped = planes[col * (PARAMS + 1) : col * (PARAMS + 1) + PARAMS, :]
        start = (col // half) * PARAMS * ROWS + col % half
        out[pl.ds(start, PARAMS, stride=ROWS), :] = jnp.where(upper, flipped, straight)


def sum_kernel(cross, arrived, out, hot, values, total, ranks):
    lines = lax.broadcasted_iota(jnp.int32, (PAIR_ORB, SLOTS), 0).astype(jnp.bfloat16)
    one = jnp.ones((PAIR_ORB, SLOTS), jnp.bfloat16)
    none = jnp.zeros((PAIR_ORB, SLOTS), jnp.bfloat16)
    total[...] = jnp.zeros_like(total)

    def body(step, carry):
        for part in range(STEP_SRC // 128):
            hots, vals = [], []
            for i in range(128):
                base = (step * STEP_SRC + part * 128 + i) * ROWS
                piece = arrived[pl.ds(base, ELEMS), :].astype(jnp.bfloat16)
                ids = arrived[pl.ds(base + ELEMS, 1), :].astype(jnp.int32)
                local = ids & (PAIR_ORB - 1)
                line = ((ids >> 8) * 32 + (local >> 6) * 8 + (local & 7)).astype(jnp.bfloat16)
                group = jnp.broadcast_to(((local >> 3) & 7).astype(jnp.bfloat16), (ELEMS, SLOTS))
                hots.append(jnp.where(lines == line, one, none))
                vals.append(jnp.concatenate([jnp.where(group == g, piece, none[:ELEMS]) for g in range(8)], axis=0))
            total[...] += dot_nt(jnp.concatenate(hots, axis=1), jnp.concatenate(vals, axis=1))
        return carry

    lax.fori_loop(0, DEVICES // STEP_SRC, body, 0)
    crossing_ranks(cross, ranks)
    for o in range(ORBITS):
        pair = pair_of(o, cross, ranks)
        for t in range(TILES):
            start = pl.multiple_of(pair * 32 + (t >> 1) * 8, 8)
            dest = (t * ORBITS + o) * 8
            out[dest : dest + 8, :] = total[pl.ds(start, 8), (t & 1) * 128 : (t & 1) * 128 + 128]


def place_kernel(cross, arrived, out, turned):
    me = lax.axis_index("orbit")
    upper = me > cross[me]
    lane = lax.broadcasted_iota(jnp.int32, (8, 128), 1)

    @pl.when(jnp.logical_not(upper))
    def _():
        band = lane // 32
        for tile in range(32):
            v = []
            for g in range(4):
                d = (g % 2) * PARAMS + 2 * tile + g // 2
                v.append(arrived[d * 8 : d * 8 + 8, :])
            moved = []
            for r in range(4):
                z = v[r]
                for h in range(1, 4):
                    z = jnp.where(band == h, v[(h + r) % 4], z)
                moved.append(z if r == 0 else pltpu.roll(z, 32 * r, 1))
            for h in range(4):
                u = moved[(0 - h) % 4]
                for g in range(1, 4):
                    u = jnp.where(band == g, moved[(g - h) % 4], u)
                start = (h * 32 + tile) * 8
                out[start : start + 8, :] = u

    @pl.when(upper)
    def _():
        low = lax.broadcasted_iota(jnp.int32, (64, 128), 1) < PARAMS
        for j in range(8):
            turned[...] = arrived[pl.ds(j, 128, stride=8), :].T
            even = turned[pl.ds(0, 64, stride=2), :]
            odd = turned[pl.ds(1, 64, stride=2), :]
            halves = (
                jnp.where(low, even, pltpu.roll(odd, PARAMS, 1)),
                jnp.where(low, pltpu.roll(even, PARAMS, 1), odd),
            )
            for h in range(4):
                for half in range(2):
                    start = h * 256 + half * 128 + j
                    out[pl.ds(start, 16, stride=8), :] = halves[half][h * 16 : h * 16 + 16]


def smem():
    return pl.BlockSpec(memory_space=pltpu.SMEM)


def exchange(x):
    return lax.all_to_all(x, ("tile", "orbit"), split_axis=0, concat_axis=0, tiled=True)


def in_vmem():
    return pl.BlockSpec(memory_space=pltpu.VMEM)


def in_hbm():
    return pl.BlockSpec(memory_space=pl.ANY)


def hbm(x):
    return pltpu.with_memory_space_constraint(x, pltpu.HBM)


def make_blocks(jacobians, point_normals, counts, owners, locals_, crossing):
    jac = jnp.transpose(jacobians, (0, 2, 1, 3)).reshape(SLOTS, 3 * PTS, 2 * PARAMS)
    normals = jnp.transpose(point_normals, (1, 0, 2))
    return pl.pallas_call(
        blocks_kernel,
        in_specs=[smem(), smem(), smem(), in_hbm(), in_hbm(), in_vmem(), in_vmem()],
        out_specs=in_vmem(),
        out_shape=pltpu.VMEM((DEVICES * ROWS, SLOTS), jnp.float32),
        scratch_shapes=[
            pltpu.VMEM((SLOTS, 3 * PTS, 2 * PARAMS), jnp.bfloat16),
            pltpu.VMEM((6, SLOTS, PTS), jnp.float32),
            pltpu.VMEM((PARAMS * (SLOTS + 1), PARAMS), jnp.float32),
            pltpu.VMEM((PARAMS * (PARAMS + 1), SLOTS), jnp.float32),
            pltpu.VMEM((STEP_SLOTS, 3, PARAMS, PTS), jnp.float32),
            pltpu.VMEM((STEP_SLOTS, 3, PARAMS, PTS), jnp.float32),
            pltpu.VMEM((STEP_SLOTS, 3, PARAMS, PTS), jnp.bfloat16),
            pltpu.VMEM((STEP_SLOTS, 3, PARAMS, PTS), jnp.bfloat16),
            pltpu.VMEM((STEP_SLOTS, 3, PARAMS, PTS), jnp.bfloat16),
            pltpu.VMEM((STEP_SLOTS, 3, PARAMS, PTS), jnp.bfloat16),
            pltpu.SMEM((ORBITS,), jnp.int32),
            pltpu.SemaphoreType.DMA((SLOTS // STEP_SLOTS + 1,)),
        ],
        compiler_params=pltpu.CompilerParams(vmem_limit_bytes=28 << 20),
        name="blocks",
    )(*map(hbm, (counts, owners, crossing, jac, normals, owners.reshape(1, SLOTS), locals_.reshape(1, SLOTS))))


def sum_pairs(arrived, crossing):
    return pl.pallas_call(
        sum_kernel,
        in_specs=[smem(), in_vmem()],
        out_specs=in_vmem(),
        out_shape=pltpu.VMEM((DEVICES * 8, 128), jnp.float32),
        scratch_shapes=[
            pltpu.VMEM((PAIR_ORB, STEP_SRC * SLOTS), jnp.bfloat16),
            pltpu.VMEM((PAIR_ORB, STEP_SRC * SLOTS), jnp.bfloat16),
            pltpu.VMEM((PAIR_ORB, PAIR_ORB), jnp.float32),
            pltpu.SMEM((ORBITS,), jnp.int32),
        ],
        compiler_params=pltpu.CompilerParams(vmem_limit_bytes=28 << 20),
        name="sum_pairs",
    )(hbm(crossing), pltpu.with_memory_space_constraint(arrived, pltpu.VMEM))


def place(arrived, crossing):
    return pl.pallas_call(
        place_kernel,
        in_specs=[smem(), in_vmem()],
        out_specs=in_vmem(),
        out_shape=jax.ShapeDtypeStruct((DEVICES * 8, 128), jnp.float32),
        scratch_shapes=[pltpu.VMEM((128, 128), jnp.float32)],
        compiler_params=pltpu.CompilerParams(vmem_limit_bytes=8 << 20),
        name="place",
    )(hbm(crossing), pltpu.with_memory_space_constraint(arrived, pltpu.VMEM))


def local(jacobians, point_normals, block_counts, pair_owner, pair_local, crossing):
    sent = make_blocks(
        jacobians, point_normals, block_counts.reshape(SLOTS), pair_owner.reshape(SLOTS), pair_local, crossing
    )
    arrived = exchange(sent.reshape(DEVICES, ROWS, 1, SLOTS))
    sums = sum_pairs(arrived.reshape(DEVICES * ROWS, SLOTS), crossing)
    mine = exchange(sums.reshape(DEVICES, 8, 128))
    out = place(mine.reshape(DEVICES * 8, 128), crossing)
    out = jnp.transpose(out.reshape(4, 32, 8, 128), (0, 2, 1, 3))
    return out.reshape(1, PAIR_ORB // TILES, PARAMS * PARAMS)


def solution(mesh):
    both = ("tile", "orbit")
    in_specs = (
        P(both, None, None, None),
        P(both, None, None),
        P(both, None),
        P(both, None),
        P(both),
        P(),
    )
    return jax.shard_map(local, mesh=mesh, in_specs=in_specs, out_specs=P("orbit", "tile", None), check_vma=False)
```
